1024 devices in a mesh: ep: 32 (over z), hd: 4 (over x), rep: 8 (over y, core).
Axes of the slice: x: 4, y: 4, z: 32, core: 2. Of those that a mesh axis runs over, the one named last changes fastest.
Arguments:
- queries: bfloat16 [1024, 64, 576], P('ep', ('hd', 'rep')), may hold values from -256 to 256
- latent_cache: bfloat16 [1024, 64, 576], P('ep'), may hold values from -6 to 6
- cached_lengths: int32 [1024], P('ep'), may hold values from 1 to 64
- prefill_rows: bfloat16 [1024, 64, 576], P('ep'), may hold values from -6 to 6
- owner_rank: int32 [1024], P('ep'), may hold values from 0 to 31, as said below
- value_up: bfloat16 [64, 512, 128], P(('hd', 'rep')), may hold values from -1 to 1
- out_proj: bfloat16 [8192, 7168], P(('hd', 'rep')), may hold values from -0.125 to 0.125
Outputs:
- mixed: bfloat16 [1024, 7168], P('ep', ('hd', 'rep'))
- fresh: bfloat16 [1024, 64, 576], P('ep', ('hd', 'rep'))
The draws below stay inside these ranges and needn't reach their ends.
Inputs may be any that keep to these rules, and one draw needn't show every extreme that they name: `owner_rank`: the 32 requests of one prefill block go to 32 different decode indices.
All inputs are finite; a program needn't handle non-finite values.
Results may differ from the reference program's by a relative error of at most 0.011.
Values may be sent and summed in bfloat16 or wider, within the bound.
No kernel may reach another device: no remote copies, remote signals or barrier semaphores. Data moves between devices by JAX's collectives and lax.ppermute only.
A program may use at most 64 MiB of HBM per device.

```python
import jax
import jax.numpy as jnp
from jax import lax

D = 7168
LAT = 512
ROPE = 64
VDIM = 128
HEADS = 64
CTX = 64
NEW = 64
REQ_DEV = 32
REQUESTS = 1024


def draw_owner_rank(key, part):
    subkeys = jax.random.split(key, REQUESTS // REQ_DEV)
    orders = jax.vmap(lambda subkey: jax.random.permutation(subkey, REQ_DEV))(subkeys)
    return orders.reshape(-1).astype(jnp.int32)


def draw_queries(key, part):
    standard = jax.random.normal(key, (REQUESTS, HEADS, LAT + ROPE), jnp.float32)
    return jnp.clip(standard, -255.0, 255.0).astype(jnp.bfloat16)


def place_ends(values, own_key, least, top_value):
    extent = values.shape
    index_at = [jax.random.randint(jax.random.fold_in(own_key, axis), (), 0, extent[axis]) for axis in range(len(extent))]
    values = values.at[tuple(index_at)].set(least)
    longest = extent.index(max(extent))
    index_at[longest] = (index_at[longest] + 1) % extent[longest]
    return values.at[tuple(index_at)].set(top_value)


def strengthened(array, rng, source, target, shards_of, factor):
    def block_of(axis_at):
        return (jnp.arange(array.shape[axis_at]) // (array.shape[axis_at] // shards_of)).reshape((-1,) + (1,) * (array.ndim - 1 - axis_at))

    near = jax.random.permutation(rng, shards_of)[block_of(target)]
    far = (block_of(target) + shards_of // 2) % shards_of
    return jnp.where((block_of(source) == near) | (block_of(source) == far), factor * array, array)


def level_of(rng, extent, cuts, smallest, largest):
    level, own = 1.0, jax.random.fold_in(rng, 6)
    for axis_at, shards_of in cuts:
        heights = jnp.exp(jax.random.uniform(jax.random.fold_in(own, axis_at), (shards_of,), jnp.float32, smallest / len(cuts), largest / len(cuts)))
        level = level * jnp.repeat(heights, extent[axis_at] // shards_of).reshape([-1 if axis == axis_at else 1 for axis in range(len(extent))])
    return level


def normal_values(own_key, dims, width, limit, pieces=(), kind=jnp.bfloat16):
    factor_of = level_of(own_key, dims, pieces, -0.22, 0.18) if pieces else 1.0
    drawn = jax.random.normal(own_key, dims, jnp.float32) * width * factor_of
    return jnp.minimum(jnp.maximum(drawn, -limit), limit).astype(kind)


def bell_draw_with(own_key, shape, scale, reach, shards, heavy, kind=jnp.bfloat16):
    result = scale * jax.random.normal(own_key, shape, jnp.float32)
    if shards:
        result = result * level_of(own_key, shape, shards, -0.22, 0.18)
    return jnp.clip(strengthened(result, jax.random.fold_in(own_key, 3), *heavy), -reach, reach).astype(kind)


def setup_inputs(seed: int = 0) -> dict:
    seeds = jax.random.split(jax.random.key(seed), 8)
    return {
        "queries": draw_queries(jax.random.fold_in(seeds[7], 71), 0),
        "latent_cache": normal_values(seeds[1], (REQUESTS, CTX, LAT + ROPE), 1.0, 6.0, ((0, 32),)),
        "cached_lengths": place_ends(jax.random.randint(seeds[2], (REQUESTS,), 1, CTX + 1), jax.random.fold_in(seeds[2], 1), 1, CTX).astype(jnp.int32),
        "prefill_rows": normal_values(seeds[3], (REQUESTS, NEW, LAT + ROPE), 1.0, 6.0, ((0, 32),)),
        "owner_rank": draw_owner_rank(jax.random.fold_in(seeds[7], 71), 0),
        "value_up": normal_values(seeds[5], (HEADS, LAT, VDIM), (LAT // 16) ** -0.5, 1.0, ((0, 32),)),
        "out_proj": bell_draw_with(seeds[6], (HEADS * VDIM, D), (HEADS * VDIM) ** -0.5, 0.125, ((0, 32),), (0, 1, 32, 2.75)),
    }


score_scale = 192.0 ** -0.5
neg_fill = -1.0e30


def route_rows(prefill_rows, owner_rank):
    flattened = prefill_rows.astype(jnp.float32).reshape(REQ_DEV, REQ_DEV, NEW * (LAT + ROPE))
    owners = owner_rank.reshape(REQ_DEV, REQ_DEV)
    choose = (owners[:, None, :] == jnp.arange(REQ_DEV, dtype=jnp.int32)[None, :, None]).astype(jnp.float32)
    delivered = jnp.einsum("sdj,sjx->dsx", choose, flattened, precision=lax.Precision.HIGHEST)
    return delivered.astype(jnp.bfloat16).reshape(REQUESTS, NEW, LAT + ROPE)


def attend(blocks):
    query_block, cache_block, length_block, fresh_rows = blocks
    keys_all = jnp.concatenate([cache_block, fresh_rows], axis=1).astype(jnp.float32)
    scores = jnp.einsum("rhk,rck->rhc", query_block.astype(jnp.float32), keys_all, precision=lax.Precision.HIGHEST) * score_scale
    position = jnp.arange(CTX + NEW, dtype=jnp.int32)
    visible = (position[None, :] < length_block[:, None]) | (position[None, :] >= CTX)
    scores = jnp.where(visible[:, None, :], scores, neg_fill)
    maxima = jnp.max(scores, axis=-1, keepdims=True)
    weights = jnp.exp(scores - maxima)
    totals = jnp.sum(weights, axis=-1, keepdims=True)
    summed = jnp.einsum("rhc,rcl->rhl", weights, keys_all[:, :, :LAT], precision=lax.Precision.HIGHEST)
    return (summed / totals).astype(jnp.bfloat16)


def reference(queries, latent_cache, cached_lengths, prefill_rows, owner_rank, value_up, out_proj):
    fresh = route_rows(prefill_rows, owner_rank)
    blocked = (
        queries.reshape(REQ_DEV, REQ_DEV, HEADS, LAT + ROPE),
        latent_cache.reshape(REQ_DEV, REQ_DEV, CTX, LAT + ROPE),
        cached_lengths.reshape(REQ_DEV, REQ_DEV),
        fresh.reshape(REQ_DEV, REQ_DEV, NEW, LAT + ROPE),
    )
    latent_out = lax.map(attend, blocked).reshape(REQUESTS, HEADS, LAT)
    head_out = jnp.einsum("rhl,hlv->rhv", latent_out.astype(jnp.float32), value_up.astype(jnp.float32), precision=lax.Precision.HIGHEST)
    head_out = head_out.astype(jnp.bfloat16).reshape(REQUESTS, HEADS * VDIM)
    mixed = jnp.dot(head_out, out_proj, preferred_element_type=jnp.float32).astype(jnp.bfloat16)
    return (mixed, fresh)
```

```python
import jax
import jax.numpy as jnp
from jax import lax
from jax.sharding import PartitionSpec as P

LAT = 512
score_scale = 192.0 ** (-0.5)
neg_fill = -1e30


def sigma(g):
    return g // 2 + 16 * (g % 2)


def body(queries, latent_cache, cached_lengths, prefill_rows, owner_rank, value_up, out_proj):
    n = latent_cache.shape[0]
    context = latent_cache.shape[1]
    width = latent_cache.shape[2]
    d = lax.axis_index("ep")
    g = lax.axis_index(("hd", "rep"))
    mine = lax.rem(sigma(g) - d + n, n)
    j = jnp.sum(jnp.where(owner_rank == mine, jnp.arange(n, dtype=jnp.int32), 0))
    row = lax.dynamic_index_in_dim(prefill_rows, j, 0, keepdims=False)
    pairs = [(s * n + k, (sigma(k) - s) % n * n + k) for s in range(n) for k in range(n)]
    fresh_row = lax.ppermute(row, ("ep", "hd", "rep"), pairs)

    seats = jnp.array([sigma(k) for k in range(n)], dtype=jnp.int32)
    request_at = lax.rem(seats - d + n, n)
    choose = (request_at[:, None] == jnp.arange(n, dtype=jnp.int32)[None, :]).astype(jnp.bfloat16)
    queries_out = jnp.einsum("gr,rhk->ghk", choose, queries, preferred_element_type=jnp.float32).astype(jnp.bfloat16)
    q = lax.all_to_all(queries_out, ("hd", "rep"), split_axis=0, concat_axis=0, tiled=True)
    q = q.reshape(-1, width)
    cache_row = lax.dynamic_index_in_dim(latent_cache, mine, 0, keepdims=False)
    length = lax.dynamic_index_in_dim(cached_lengths, mine, 0, keepdims=False)
    keys = jnp.concatenate([cache_row, fresh_row], axis=0)
    scores = jnp.einsum("hk,ck->hc", q, keys, preferred_element_type=jnp.float32) * score_scale
    position = jnp.arange(keys.shape[0], dtype=jnp.int32)
    visible = (position < length) | (position >= context)
    scores = jnp.where(visible[None, :], scores, neg_fill)
    maxima = jnp.max(scores, axis=-1, keepdims=True)
    weights = jnp.exp(scores - maxima)
    totals = jnp.sum(weights, axis=-1, keepdims=True)
    summed = jnp.einsum("hc,cl->hl", weights, keys[:, :LAT], preferred_element_type=jnp.float32)
    latent = (summed / totals).astype(jnp.bfloat16)
    latent = jnp.pad(latent, ((0, 0), (0, width - LAT)))
    both = jnp.concatenate([latent.reshape(n, 2, width), fresh_row.reshape(n, 2, width)], axis=1)
    both = lax.all_to_all(both, ("hd", "rep"), split_axis=0, concat_axis=0, tiled=True)
    both = jnp.einsum("gr,ghk->rhk", choose, both, preferred_element_type=jnp.float32).astype(jnp.bfloat16)
    latent_out = both[:, :2, :LAT]
    fresh = both[:, 2:, :]
    head_out = jnp.einsum("rhl,hlv->rhv", latent_out, value_up, preferred_element_type=jnp.float32)
    head_out = head_out.astype(jnp.bfloat16).reshape(n, -1)
    partial_term = jnp.dot(head_out, out_proj, preferred_element_type=jnp.float32).astype(jnp.bfloat16)
    parts = jnp.moveaxis(partial_term.reshape(n, n, -1), 1, 0)
    arrived = lax.all_to_all(parts, ("hd", "rep"), split_axis=0, concat_axis=0, tiled=True)
    mixed = arrived.astype(jnp.float32).sum(axis=0).astype(jnp.bfloat16)
    return (mixed, fresh)


def solution(mesh):
    in_specs = (
        P("ep", ("hd", "rep"), None),
        P("ep", None, None),
        P("ep"),
        P("ep", None, None),
        P("ep"),
        P(("hd", "rep"), None, None),
        P(("hd", "rep"), None),
    )
    out_specs = (P("ep", ("hd", "rep")), P("ep", ("hd", "rep"), None))
    return jax.shard_map(body, mesh=mesh, in_specs=in_specs, out_specs=out_specs, check_vma=False)
```

```python
import jax
import jax.numpy as jnp
from jax import lax
from jax.experimental import pallas as pl
from jax.experimental.pallas import tpu as pltpu
from jax.sharding import PartitionSpec as P


LAT = 512
score_scale = 192.0 ** (-0.5)
neg_fill = -1e30


def sigma(g):
    return g // 2 + 16 * (g % 2)


def seat_request(n):
    d = lax.axis_index("ep")
    g = lax.axis_index("hd") * lax.axis_size("rep") + lax.axis_index("rep")
    return lax.rem(lax.div(g, 2) + (n // 2) * lax.rem(g, 2) - d + n, n)


def pick_kernel(owner_ref, rows_ref, after_ref, row_ref, sem):
    n = rows_ref.shape[0]
    mine = seat_request(n)
    j = jnp.int32(0)
    for i in range(n):
        j = jnp.where(owner_ref[i] == mine, jnp.int32(i), j)
    copy = pltpu.make_async_copy(rows_ref.at[j], row_ref, sem)
    copy.start()
    copy.wait()


def pick_row(owner_rank, prefill_rows, after):
    return pl.pallas_call(
        pick_kernel,
        out_shape=jax.ShapeDtypeStruct(prefill_rows.shape[1:], prefill_rows.dtype),
        in_specs=[
            pl.BlockSpec(memory_space=pltpu.SMEM),
            pl.BlockSpec(memory_space=pl.ANY),
            pl.BlockSpec(memory_space=pl.ANY),
        ],
        out_specs=pl.BlockSpec(memory_space=pltpu.VMEM),
        scratch_shapes=[pltpu.SemaphoreType.DMA],
        name="pick_row",
    )(owner_rank, prefill_rows, after)


def body(queries, latent_cache, cached_lengths, prefill_rows, owner_rank, value_up, out_proj):
    n = latent_cache.shape[0]
    context = latent_cache.shape[1]
    width = latent_cache.shape[2]
    d = lax.axis_index("ep")
    mine = seat_request(n)
    pairs = [(s * n + k, (sigma(k) - s) % n * n + k) for s in range(n) for k in range(n)]
    seats = jnp.array([sigma(k) for k in range(n)], dtype=jnp.int32)

    def choice():
        request_at = lax.rem(seats - d + n, n)
        return (request_at[:, None] == jnp.arange(n, dtype=jnp.int32)[None, :]).astype(jnp.bfloat16)

    def spread(value):
        ordered = jnp.einsum("gr,rhk->ghk", choice(), value, preferred_element_type=jnp.float32)
        return lax.all_to_all(
            ordered.astype(jnp.bfloat16), ("hd", "rep"), split_axis=0, concat_axis=0, tiled=True
        )

    early = (d <= 9) | (d >= 26)
    q_first = lax.cond(early, spread, lambda value: jnp.zeros_like(value), queries)
    row = pick_row(owner_rank, prefill_rows, q_first)
    fresh_row = lax.ppermute(row, ("ep", "hd", "rep"), pairs)
    q = lax.cond(early, lambda had, value: had, lambda had, value: spread(value), q_first, queries)
    q = q.reshape(-1, width)
    choose = choice()
    cache_row = lax.dynamic_index_in_dim(latent_cache, mine, 0, keepdims=False)
    length = lax.dynamic_index_in_dim(cached_lengths, mine, 0, keepdims=False)
    keys = jnp.concatenate([cache_row, fresh_row], axis=0)
    scores = jnp.einsum("hk,ck->hc", q, keys, preferred_element_type=jnp.float32) * score_scale
    position = jnp.arange(keys.shape[0], dtype=jnp.int32)
    visible = (position < length) | (position >= context)
    scores = jnp.where(visible[None, :], scores, neg_fill)
    maxima = jnp.max(scores, axis=-1, keepdims=True)
    weights = jnp.exp(scores - maxima)
    totals = jnp.sum(weights, axis=-1, keepdims=True)
    summed = jnp.einsum("hc,cl->hl", weights, keys[:, :LAT], preferred_element_type=jnp.float32)
    latent = (summed / totals).astype(jnp.bfloat16)
    latent = jnp.pad(latent, ((0, 0), (0, width - LAT)))
    both = jnp.concatenate([latent.reshape(n, 2, width), fresh_row.reshape(n, 2, width)], axis=1)
    both = lax.all_to_all(both, ("hd", "rep"), split_axis=0, concat_axis=0, tiled=True)
    both = jnp.einsum("gr,ghk->rhk", choose, both, preferred_element_type=jnp.float32).astype(jnp.bfloat16)
    latent_out = both[:, :2, :LAT]
    fresh = both[:, 2:, :]
    head_out = jnp.einsum("rhl,hlv->rhv", latent_out, value_up, preferred_element_type=jnp.float32)
    head_out = head_out.astype(jnp.bfloat16).reshape(n, -1)
    partial_term = jnp.dot(head_out, out_proj, preferred_element_type=jnp.float32).astype(jnp.bfloat16)
    parts = jnp.moveaxis(partial_term.reshape(n, n, -1), 1, 0)
    arrived = lax.all_to_all(parts, ("hd", "rep"), split_axis=0, concat_axis=0, tiled=True)
    mixed = arrived.astype(jnp.float32).sum(axis=0).astype(jnp.bfloat16)
    return (mixed, fresh)


def solution(mesh):
    in_specs = (
        P("ep", ("hd", "rep"), None),
        P("ep", None, None),
        P("ep"),
        P("ep", None, None),
        P("ep"),
        P(("hd", "rep"), None, None),
        P(("hd", "rep"), None),
    )
    out_specs = (P("ep", ("hd", "rep")), P("ep", ("hd", "rep"), None))

    return jax.shard_map(body, mesh=mesh, in_specs=in_specs, out_specs=out_specs, check_vma=False)
```

```python
import jax
import jax.numpy as jnp
from jax import lax
from jax.experimental import pallas as pl
from jax.experimental.pallas import tpu as pltpu
from jax.sharding import PartitionSpec as P


LAT = 512
score_scale = 192.0 ** (-0.5)
neg_fill = -1e30
VMEM = pl.BlockSpec(memory_space=pltpu.VMEM)
SMEM = pl.BlockSpec(memory_space=pltpu.SMEM)
ANY = pl.BlockSpec(memory_space=pl.ANY)


def sigma(g):
    return g // 2 + 16 * (g % 2)


def seat_request(n):
    d = lax.axis_index("ep")
    g = lax.axis_index("hd") * lax.axis_size("rep") + lax.axis_index("rep")
    return lax.rem(lax.div(g, 2) + (n // 2) * lax.rem(g, 2) - d + n, n)


def leaving(z, n):
    half = n // 2
    rank = 12 * z * (z <= half) + (12 * half - 5 * (z - half)) * (z > half)
    return rank * n + z


def pick_kernel(owner_ref, rows_ref, row_ref, sem):
    n = rows_ref.shape[0]
    mine = seat_request(n)
    j = jnp.int32(0)
    for i in range(n):
        j = jnp.where(owner_ref[i] == mine, jnp.int32(i), j)
    copy = pltpu.make_async_copy(rows_ref.at[j], row_ref, sem)
    copy.start()
    copy.wait()


def pick_row(owner_rank, prefill_rows):
    return pl.pallas_call(
        pick_kernel,
        out_shape=jax.ShapeDtypeStruct(prefill_rows.shape[1:], prefill_rows.dtype),
        in_specs=[SMEM, ANY],
        out_specs=VMEM,
        scratch_shapes=[pltpu.SemaphoreType.DMA],
        name="pick_row",
    )(owner_rank, prefill_rows)


def cached_kernel(lengths_ref, cache_ref, row_ref, bias_ref, sem):
    mine = seat_request(cache_ref.shape[0])
    copy = pltpu.make_async_copy(cache_ref.at[mine], row_ref, sem)
    copy.start()
    position = lax.broadcasted_iota(jnp.int32, bias_ref.shape, 1)
    visible = (position < lengths_ref[mine]) | (position >= cache_ref.shape[1])
    bias_ref[...] = jnp.where(visible, 0.0, neg_fill)
    copy.wait()


def pick_cached(cached_lengths, latent_cache, positions):
    return pl.pallas_call(
        cached_kernel,
        out_shape=(
            jax.ShapeDtypeStruct(latent_cache.shape[1:], latent_cache.dtype),
            jax.ShapeDtypeStruct((8, positions), jnp.float32),
        ),
        in_specs=[SMEM, ANY],
        out_specs=(VMEM, VMEM),
        scratch_shapes=[pltpu.SemaphoreType.DMA],
        name="pick_cached",
    )(cached_lengths, latent_cache)


def project_kernel(latent_ref, up_ref, out_proj_ref, parts_ref, weights, sems):
    _, _, columns = parts_ref.shape
    steps, _, wide = weights.shape
    each = wide // columns
    copies = []
    for i in range(steps):
        window = out_proj_ref.at[:, pl.ds(i * wide, wide)]
        copies.append(pltpu.make_async_copy(window, weights.at[i], sems.at[i]))
        copies[i].start()
    heads = [
        jnp.dot(latent_ref[i, :, :LAT], up_ref[i], preferred_element_type=jnp.float32)
        for i in range(up_ref.shape[0])
    ]
    head_out = jnp.concatenate(heads, axis=1).astype(jnp.bfloat16)
    for i in range(steps):
        copies[i].wait()
        term = jnp.dot(head_out, weights[i], preferred_element_type=jnp.float32)
        for k in range(each):
            piece = term[:, k * columns : (k + 1) * columns]
            parts_ref[each * i + k] = piece.astype(jnp.bfloat16)


def project(latent, value_up, out_proj, n):
    depth, width = out_proj.shape
    steps = n // 4
    return pl.pallas_call(
        project_kernel,
        out_shape=jax.ShapeDtypeStruct((n, latent.shape[1], width // n), jnp.bfloat16),
        in_specs=[VMEM, VMEM, ANY],
        out_specs=VMEM,
        scratch_shapes=[
            pltpu.VMEM((steps, depth, width // steps), jnp.bfloat16),
            pltpu.SemaphoreType.DMA((steps,)),
        ],
        cost_estimate=pl.CostEstimate(
            flops=2 * latent.shape[1] * depth * width,
            bytes_accessed=2 * depth * width,
            transcendentals=0,
        ),
        name="project",
    )(latent, value_up, out_proj)


def body(queries, latent_cache, cached_lengths, prefill_rows, owner_rank, value_up, out_proj):
    n = latent_cache.shape[0]
    width = latent_cache.shape[2]
    positions = latent_cache.shape[1] + prefill_rows.shape[1]
    d = lax.axis_index("ep")
    mine = seat_request(n)
    later, sooner = [], []
    for source in range(n):
        for k in range(n):
            owner = (sigma(k) - source) % n
            pair = (source * n + k, owner * n + k)
            (later if leaving(source, n) >= leaving(owner, n) else sooner).append(pair)
    from_later = leaving(mine, n) >= leaving(d, n)
    seats = jnp.array([sigma(k) for k in range(n)], dtype=jnp.int32)

    def choice():
        request_at = lax.rem(seats - d + n, n)
        return (request_at[:, None] == jnp.arange(n, dtype=jnp.int32)[None, :]).astype(jnp.bfloat16)

    def prepare(queries, cached_lengths, latent_cache):
        ordered = jnp.einsum("gr,rhk->ghk", choice(), queries, preferred_element_type=jnp.float32)
        q = lax.all_to_all(
            ordered.astype(jnp.bfloat16), ("hd", "rep"), split_axis=0, concat_axis=0, tiled=True
        )
        cache_row, bias = pick_cached(cached_lengths, latent_cache, positions)
        return q.reshape(-1, width), cache_row, bias

    def nothing(queries, cached_lengths, latent_cache):
        return (
            jnp.zeros((queries.shape[1] * n, width), queries.dtype),
            jnp.zeros(latent_cache.shape[1:], latent_cache.dtype),
            jnp.zeros((8, positions), jnp.float32),
        )

    early = (d <= 9 * n // 32) | (d >= 26 * n // 32)
    row = pick_row(owner_rank, prefill_rows)
    operands = (queries, cached_lengths, latent_cache)
    late_row = lax.ppermute(row, ("ep", "hd", "rep"), later)
    had = lax.cond(early, prepare, nothing, *operands)
    early_row = lax.ppermute(row, ("ep", "hd", "rep"), sooner)
    q, cache_row, bias = lax.cond(
        early, lambda had, operands: had, lambda had, operands: prepare(*operands), had, operands
    )
    fresh_row = jnp.where(from_later, late_row, early_row)
    keys = jnp.concatenate([cache_row, fresh_row], axis=0)
    scores = jnp.einsum("hk,ck->hc", q, keys, preferred_element_type=jnp.float32) * score_scale
    scores = scores + bias[:1]
    maxima = jnp.max(scores, axis=-1, keepdims=True)
    weights = jnp.exp(scores - maxima)
    totals = jnp.sum(weights, axis=-1, keepdims=True)
    summed = jnp.einsum("hc,cl->hl", weights, keys[:, :LAT], preferred_element_type=jnp.float32)
    latent = (summed / totals).astype(jnp.bfloat16)
    latent = jnp.pad(latent, ((0, 0), (0, width - LAT)))
    both = jnp.concatenate([latent.reshape(n, 2, width), fresh_row.reshape(n, 2, width)], axis=1)
    both = lax.all_to_all(both, ("hd", "rep"), split_axis=0, concat_axis=0, tiled=True)
    both = jnp.einsum("gr,ghk->rhk", choice(), both, preferred_element_type=jnp.float32)
    both = both.astype(jnp.bfloat16)
    fresh = both[:, 2:, :]
    parts = project(jnp.moveaxis(both, 1, 0), value_up, out_proj, n)
    arrived = lax.all_to_all(parts, ("hd", "rep"), split_axis=0, concat_axis=0, tiled=True)
    mixed = arrived.astype(jnp.float32).sum(axis=0).astype(jnp.bfloat16)
    return (mixed, fresh)


def solution(mesh):
    in_specs = (
        P("ep", ("hd", "rep"), None),
        P("ep", None, None),
        P("ep"),
        P("ep", None, None),
        P("ep"),
        P(("hd", "rep"), None, None),
        P(("hd", "rep"), None),
    )
    out_specs = (P("ep", ("hd", "rep")), P("ep", ("hd", "rep"), None))

    return jax.shard_map(body, mesh=mesh, in_specs=in_specs, out_specs=out_specs, check_vma=False)
```

```python
import jax
import jax.numpy as jnp
from jax import lax
from jax.experimental import pallas as pl
from jax.experimental.pallas import tpu as pltpu
from jax.sharding import PartitionSpec as P


LAT = 512
score_scale = 192.0 ** (-0.5)
neg_fill = -1e30
GRANT = 64_720_000
VMEM = pl.BlockSpec(memory_space=pltpu.VMEM)
SMEM = pl.BlockSpec(memory_space=pltpu.SMEM)
HBM = pl.BlockSpec(memory_space=pltpu.HBM)


def sigma(g, n=32):
    return (n // 4 + (g // 2 + n // 4) % (n // 2) + n // 2 * (g % 2)) % n


def seat_request(n):
    d = lax.axis_index("ep")
    g = lax.axis_index("hd") * lax.axis_size("rep") + lax.axis_index("rep")
    seat = n // 4 + lax.rem(lax.div(g, 2) + n // 4, n // 2) + (n // 2) * lax.rem(g, 2)
    return lax.rem(seat - d + n, n)


def leaving(z, n):
    half = n // 2
    rank = 12 * z * (z <= half) + (12 * half - 5 * (z - half)) * (z > half)
    return rank * n + z


def pick_kernel(owner_ref, rows_ref, row_ref, sem):
    n = rows_ref.shape[0]
    mine = seat_request(n)
    j = jnp.int32(0)
    for i in range(n):
        j = jnp.where(owner_ref[i] == mine, jnp.int32(i), j)
    copy = pltpu.make_async_copy(rows_ref.at[j], row_ref, sem)
    copy.start()
    copy.wait()


def pick_row(owner_rank, prefill_rows):
    return pl.pallas_call(
        pick_kernel,
        out_shape=jax.ShapeDtypeStruct(prefill_rows.shape[1:], prefill_rows.dtype),
        in_specs=[SMEM, HBM],
        out_specs=VMEM,
        scratch_shapes=[pltpu.SemaphoreType.DMA],
        compiler_params=pltpu.CompilerParams(vmem_limit_bytes=GRANT),
        name="pick_row",
    )(owner_rank, prefill_rows)


def cached_kernel(lengths_ref, cache_ref, row_ref, bias_ref, sem):
    mine = seat_request(cache_ref.shape[0])
    copy = pltpu.make_async_copy(cache_ref.at[mine], row_ref, sem)
    copy.start()
    position = lax.broadcasted_iota(jnp.int32, bias_ref.shape, 1)
    visible = (position < lengths_ref[mine]) | (position >= cache_ref.shape[1])
    bias_ref[...] = jnp.where(visible, 0.0, neg_fill)
    copy.wait()


def pick_cached(cached_lengths, latent_cache, positions):
    return pl.pallas_call(
        cached_kernel,
        out_shape=(
            jax.ShapeDtypeStruct(latent_cache.shape[1:], latent_cache.dtype),
            jax.ShapeDtypeStruct((8, positions), jnp.float32),
        ),
        in_specs=[SMEM, HBM],
        out_specs=(VMEM, VMEM),
        scratch_shapes=[pltpu.SemaphoreType.DMA],
        compiler_params=pltpu.CompilerParams(vmem_limit_bytes=GRANT),
        name="pick_cached",
    )(cached_lengths, latent_cache)


def project_kernel(both_ref, up_ref, out_proj_ref, parts_ref, weights, sems):
    n, _, columns = parts_ref.shape
    steps, _, wide = weights.shape
    copies = []
    for i in range(steps):
        window = out_proj_ref.at[:, pl.ds(i * wide, wide)]
        copies.append(pltpu.make_async_copy(window, weights.at[i], sems.at[i]))
        copies[i].start()
    d = lax.axis_index("ep")
    both = both_ref[...]
    heads = [
        jnp.dot(both[:, i, :LAT], up_ref[i], preferred_element_type=jnp.float32)
        for i in range(up_ref.shape[0])
    ]
    head_out = jnp.concatenate(heads, axis=1).astype(jnp.bfloat16)
    seat = lax.broadcasted_iota(jnp.int32, (n, n), 1)
    request = lax.broadcasted_iota(jnp.int32, (n, n), 0)
    chip, core = lax.shift_right_logical(seat, 1), lax.bitwise_and(seat, 1)
    seat = n // 4 + lax.bitwise_and(chip + n // 4, n // 2 - 1) + (n // 2) * core
    choose = lax.bitwise_and(request + d - seat, n - 1) == 0
    choose = jnp.where(choose, 1.0, 0.0).astype(jnp.bfloat16)
    head_out = jnp.dot(choose, head_out, preferred_element_type=jnp.float32).astype(jnp.bfloat16)
    each = wide // columns
    for i in range(steps):
        copies[i].wait()
        term = jnp.dot(head_out, weights[i], preferred_element_type=jnp.float32)
        for k in range(each):
            piece = term[:, k * columns : (k + 1) * columns]
            parts_ref[each * i + k] = piece.astype(jnp.bfloat16)


def project(both, value_up, out_proj):
    n = both.shape[0]
    depth, width = out_proj.shape
    return pl.pallas_call(
        project_kernel,
        out_shape=jax.ShapeDtypeStruct((n, n, width // n), jnp.bfloat16),
        in_specs=[VMEM, VMEM, HBM],
        out_specs=VMEM,
        scratch_shapes=[
            pltpu.VMEM((n // 4, depth, 4 * width // n), jnp.bfloat16),
            pltpu.SemaphoreType.DMA((n // 4,)),
        ],
        compiler_params=pltpu.CompilerParams(vmem_limit_bytes=GRANT),
        cost_estimate=pl.CostEstimate(
            flops=2 * n * depth * width, bytes_accessed=2 * depth * width, transcendentals=0
        ),
        name="project",
    )(both, value_up, out_proj)


def body(queries, latent_cache, cached_lengths, prefill_rows, owner_rank, value_up, out_proj):
    n = latent_cache.shape[0]
    width = latent_cache.shape[2]
    positions = latent_cache.shape[1] + prefill_rows.shape[1]
    d = lax.axis_index("ep")
    mine = seat_request(n)
    later, sooner = [], []
    for source in range(n):
        for k in range(n):
            owner = (sigma(k) - source) % n
            pair = (source * n + k, owner * n + k)
            (later if leaving(source, n) >= leaving(owner, n) else sooner).append(pair)
    from_later = leaving(mine, n) >= leaving(d, n)
    seats = jnp.array([sigma(k) for k in range(n)], dtype=jnp.int32)

    def choice():
        request_at = lax.rem(seats - d + n, n)
        return (request_at[:, None] == jnp.arange(n, dtype=jnp.int32)[None, :]).astype(jnp.bfloat16)

    def prepare(queries, cached_lengths, latent_cache):
        ordered = jnp.einsum("gr,rhk->ghk", choice(), queries, preferred_element_type=jnp.float32)
        q = lax.all_to_all(
            ordered.astype(jnp.bfloat16), ("hd", "rep"), split_axis=0, concat_axis=0, tiled=True
        )
        cache_row, bias = pick_cached(cached_lengths, latent_cache, positions)
        return q.reshape(-1, width), cache_row, bias

    def nothing(queries, cached_lengths, latent_cache):
        return (
            jnp.zeros((queries.shape[1] * n, width), queries.dtype),
            jnp.zeros(latent_cache.shape[1:], latent_cache.dtype),
            jnp.zeros((8, positions), jnp.float32),
        )

    early = (d < 12 * n // 32) | (d >= 28 * n // 32)
    row = pick_row(owner_rank, prefill_rows)
    operands = (queries, cached_lengths, latent_cache)
    late_row = lax.ppermute(row, ("ep", "hd", "rep"), later)
    had = lax.cond(early, prepare, nothing, *operands)
    early_row = lax.ppermute(row, ("ep", "hd", "rep"), sooner)
    q, cache_row, bias = lax.cond(
        early, lambda had, operands: had, lambda had, operands: prepare(*operands), had, operands
    )
    fresh_row = jnp.where(from_later, late_row, early_row)
    keys = jnp.concatenate([cache_row, fresh_row], axis=0)
    scores = jnp.einsum("hk,ck->hc", q, keys, preferred_element_type=jnp.float32) * score_scale
    scores = scores + bias[:1]
    maxima = jnp.max(scores, axis=-1, keepdims=True)
    weights = jnp.exp(scores - maxima)
    totals = jnp.sum(weights, axis=-1, keepdims=True)
    summed = jnp.einsum("hc,cl->hl", weights, keys[:, :LAT], preferred_element_type=jnp.float32)
    latent = (summed / totals).astype(jnp.bfloat16)
    latent = jnp.pad(latent, ((0, 0), (0, width - LAT)))
    both = jnp.concatenate([latent.reshape(n, 2, width), fresh_row.reshape(n, 2, width)], axis=1)
    both = lax.all_to_all(both, ("hd", "rep"), split_axis=0, concat_axis=0, tiled=True)
    parts = project(both, value_up, out_proj)
    arrived = lax.all_to_all(parts, ("hd", "rep"), split_axis=0, concat_axis=0, tiled=True)
    fresh = jnp.einsum("gr,ghk->rhk", choice(), both[:, 2:, :], preferred_element_type=jnp.float32)
    fresh = fresh.astype(jnp.bfloat16)
    mixed = arrived.astype(jnp.float32).sum(axis=0).astype(jnp.bfloat16)
    return (mixed, fresh)


def solution(mesh):
    in_specs = (
        P("ep", ("hd", "rep"), None),
        P("ep", None, None),
        P("ep"),
        P("ep", None, None),
        P("ep"),
        P(("hd", "rep"), None, None),
        P(("hd", "rep"), None),
    )
    out_specs = (P("ep", ("hd", "rep")), P("ep", ("hd", "rep"), None))

    return jax.shard_map(body, mesh=mesh, in_specs=in_specs, out_specs=out_specs, check_vma=False)
```

```python
import jax
import jax.numpy as jnp
from jax import lax
from jax.experimental import pallas as pl
from jax.experimental.pallas import tpu as pltpu
from jax.sharding import PartitionSpec as P


LAT = 512
score_scale = 192.0 ** (-0.5)
neg_fill = -1e30
GRANT = 64_720_000
VMEM = pl.BlockSpec(memory_space=pltpu.VMEM)
SMEM = pl.BlockSpec(memory_space=pltpu.SMEM)
HBM = pl.BlockSpec(memory_space=pltpu.HBM)


def sigma(g, n=32):
    return (n // 4 + g // 2 + n // 2 * (g % 2)) % n


def seat_request(n):
    d = lax.axis_index("ep")
    g = lax.axis_index("hd") * lax.axis_size("rep") + lax.axis_index("rep")
    seat = n // 4 + lax.div(g, 2) + (n // 2) * lax.rem(g, 2)
    return lax.rem(seat - d + n, n)


def leaving(z, n):
    half = n // 2
    rank = 12 * z * (z <= half) + (12 * half - 5 * (z - half)) * (z > half)
    return rank * n + z


def pick_kernel(owner_ref, rows_ref, row_ref, sem):
    n = rows_ref.shape[0]
    mine = seat_request(n)
    j = jnp.int32(0)
    for i in range(n):
        j = jnp.where(owner_ref[i] == mine, jnp.int32(i), j)
    copy = pltpu.make_async_copy(rows_ref.at[j], row_ref, sem)
    copy.start()
    copy.wait()


def pick_row(owner_rank, prefill_rows):
    return pl.pallas_call(
        pick_kernel,
        out_shape=jax.ShapeDtypeStruct(prefill_rows.shape[1:], prefill_rows.dtype),
        in_specs=[SMEM, HBM],
        out_specs=VMEM,
        scratch_shapes=[pltpu.SemaphoreType.DMA],
        compiler_params=pltpu.CompilerParams(vmem_limit_bytes=GRANT),
        name="pick_row",
    )(owner_rank, prefill_rows)


def cached_kernel(lengths_ref, cache_ref, row_ref, bias_ref, sem):
    mine = seat_request(cache_ref.shape[0])
    copy = pltpu.make_async_copy(cache_ref.at[mine], row_ref, sem)
    copy.start()
    position = lax.broadcasted_iota(jnp.int32, bias_ref.shape, 1)
    visible = (position < lengths_ref[mine]) | (position >= cache_ref.shape[1])
    bias_ref[...] = jnp.where(visible, 0.0, neg_fill)
    copy.wait()


def pick_cached(cached_lengths, latent_cache, positions):
    return pl.pallas_call(
        cached_kernel,
        out_shape=(
            jax.ShapeDtypeStruct(latent_cache.shape[1:], latent_cache.dtype),
            jax.ShapeDtypeStruct((8, positions), jnp.float32),
        ),
        in_specs=[SMEM, HBM],
        out_specs=(VMEM, VMEM),
        scratch_shapes=[pltpu.SemaphoreType.DMA],
        compiler_params=pltpu.CompilerParams(vmem_limit_bytes=GRANT),
        name="pick_cached",
    )(cached_lengths, latent_cache)


def project_kernel(both_ref, up_ref, out_proj_ref, parts_ref, weights, sems):
    n, _, columns = parts_ref.shape
    steps, _, wide = weights.shape
    copies = []
    for i in range(steps):
        window = out_proj_ref.at[:, pl.ds(i * wide, wide)]
        copies.append(pltpu.make_async_copy(window, weights.at[i], sems.at[i]))
        copies[i].start()
    d = lax.axis_index("ep")
    both = both_ref[...]
    heads = [
        jnp.dot(both[:, i, :LAT], up_ref[i], preferred_element_type=jnp.float32)
        for i in range(up_ref.shape[0])
    ]
    head_out = jnp.concatenate(heads, axis=1).astype(jnp.bfloat16)
    seat = lax.broadcasted_iota(jnp.int32, (n, n), 1)
    request = lax.broadcasted_iota(jnp.int32, (n, n), 0)
    chip, core = lax.shift_right_logical(seat, 1), lax.bitwise_and(seat, 1)
    seat = n // 4 + chip + (n // 2) * core
    choose = lax.bitwise_and(request + d - seat, n - 1) == 0
    choose = jnp.where(choose, 1.0, 0.0).astype(jnp.bfloat16)
    head_out = jnp.dot(choose, head_out, preferred_element_type=jnp.float32).astype(jnp.bfloat16)
    each = wide // columns
    for i in range(steps):
        copies[i].wait()
        term = jnp.dot(head_out, weights[i], preferred_element_type=jnp.float32)
        for k in range(each):
            piece = term[:, k * columns : (k + 1) * columns]
            parts_ref[each * i + k] = piece.astype(jnp.bfloat16)


def project(both, value_up, out_proj):
    n = both.shape[0]
    depth, width = out_proj.shape
    return pl.pallas_call(
        project_kernel,
        out_shape=jax.ShapeDtypeStruct((n, n, width // n), jnp.bfloat16),
        in_specs=[VMEM, VMEM, HBM],
        out_specs=VMEM,
        scratch_shapes=[
            pltpu.VMEM((n // 4, depth, 4 * width // n), jnp.bfloat16),
            pltpu.SemaphoreType.DMA((n // 4,)),
        ],
        compiler_params=pltpu.CompilerParams(vmem_limit_bytes=63_600_000),
        cost_estimate=pl.CostEstimate(
            flops=2 * n * depth * width, bytes_accessed=2 * depth * width, transcendentals=0
        ),
        name="project",
    )(both, value_up, out_proj)


def body(queries, latent_cache, cached_lengths, prefill_rows, owner_rank, value_up, out_proj):
    n = latent_cache.shape[0]
    width = latent_cache.shape[2]
    positions = latent_cache.shape[1] + prefill_rows.shape[1]
    d = lax.axis_index("ep")
    mine = seat_request(n)
    later, sooner = [], []
    for source in range(n):
        for k in range(n):
            owner = (sigma(k) - source) % n
            pair = (source * n + k, owner * n + k)
            (later if leaving(source, n) >= leaving(owner, n) else sooner).append(pair)
    from_later = leaving(mine, n) >= leaving(d, n)
    seats = jnp.array([sigma(k) for k in range(n)], dtype=jnp.int32)

    def choice():
        request_at = lax.rem(seats - d + n, n)
        return (request_at[:, None] == jnp.arange(n, dtype=jnp.int32)[None, :]).astype(jnp.bfloat16)

    def prepare(queries, cached_lengths, latent_cache):
        ordered = jnp.einsum("gr,rhk->ghk", choice(), queries, preferred_element_type=jnp.float32)
        q = lax.all_to_all(
            ordered.astype(jnp.bfloat16), ("hd", "rep"), split_axis=0, concat_axis=0, tiled=True
        )
        cache_row, bias = pick_cached(cached_lengths, latent_cache, positions)
        return q.reshape(-1, width), cache_row, bias

    def nothing(queries, cached_lengths, latent_cache):
        return (
            jnp.zeros((queries.shape[1] * n, width), queries.dtype),
            jnp.zeros(latent_cache.shape[1:], latent_cache.dtype),
            jnp.zeros((8, positions), jnp.float32),
        )

    early = d < n // 4
    row = pick_row(owner_rank, prefill_rows)
    operands = (queries, cached_lengths, latent_cache)
    late_row = lax.ppermute(row, ("ep", "hd", "rep"), later)
    had = lax.cond(early, prepare, nothing, *operands)
    early_row = lax.ppermute(row, ("ep", "hd", "rep"), sooner)
    q, cache_row, bias = lax.cond(
        early, lambda had, operands: had, lambda had, operands: prepare(*operands), had, operands
    )
    fresh_row = jnp.where(from_later, late_row, early_row)
    keys = jnp.concatenate([cache_row, fresh_row], axis=0)
    scores = jnp.einsum("hk,ck->hc", q, keys, preferred_element_type=jnp.float32) * score_scale
    scores = scores + bias[:1]
    maxima = jnp.max(scores, axis=-1, keepdims=True)
    weights = jnp.exp(scores - maxima)
    totals = jnp.sum(weights, axis=-1, keepdims=True)
    summed = jnp.einsum("hc,cl->hl", weights, keys[:, :LAT], preferred_element_type=jnp.float32)
    latent = (summed / totals).astype(jnp.bfloat16)
    latent = jnp.pad(latent, ((0, 0), (0, width - LAT)))
    both = jnp.concatenate([latent.reshape(n, 2, width), fresh_row.reshape(n, 2, width)], axis=1)
    both = lax.all_to_all(both, ("hd", "rep"), split_axis=0, concat_axis=0, tiled=True)
    parts = project(both, value_up, out_proj)
    arrived = lax.all_to_all(parts, ("hd", "rep"), split_axis=0, concat_axis=0, tiled=True)
    fresh = jnp.einsum("gr,ghk->rhk", choice(), both[:, 2:, :], preferred_element_type=jnp.float32)
    fresh = fresh.astype(jnp.bfloat16)
    mixed = arrived.astype(jnp.float32).sum(axis=0).astype(jnp.bfloat16)
    return (mixed, fresh)


def solution(mesh):
    in_specs = (
        P("ep", ("hd", "rep"), None),
        P("ep", None, None),
        P("ep"),
        P("ep", None, None),
        P("ep"),
        P(("hd", "rep"), None, None),
        P(("hd", "rep"), None),
    )
    out_specs = (P("ep", ("hd", "rep")), P("ep", ("hd", "rep"), None))

    return jax.shard_map(body, mesh=mesh, in_specs=in_specs, out_specs=out_specs, check_vma=False)
```

```python
import jax
import jax.numpy as jnp
from jax import lax
from jax.experimental import pallas as pl
from jax.experimental.pallas import tpu as pltpu
from jax.sharding import PartitionSpec as P


LAT = 512
score_scale = 192.0 ** (-0.5)
neg_fill = -1e30
GRANT = 64_720_000
VMEM = pl.BlockSpec(memory_space=pltpu.VMEM)
SMEM = pl.BlockSpec(memory_space=pltpu.SMEM)
HBM = pl.BlockSpec(memory_space=pltpu.HBM)


def sigma(g, n=32):
    return (n // 4 + g // 2 + n // 2 * (g % 2)) % n


def seat_request(n):
    d = lax.axis_index("ep")
    g = lax.axis_index("hd") * lax.axis_size("rep") + lax.axis_index("rep")
    seat = n // 4 + lax.div(g, 2) + (n // 2) * lax.rem(g, 2)
    return lax.rem(seat - d + n, n)


def leaving(z, n):
    half = n // 2
    rank = 12 * z * (z <= half) + (12 * half - 5 * (z - half)) * (z > half)
    return rank * n + z


def pick_kernel(owner_ref, rows_ref, row_ref, sem):
    n = rows_ref.shape[0]
    mine = seat_request(n)
    j = jnp.int32(0)
    for i in range(n):
        j = jnp.where(owner_ref[i] == mine, jnp.int32(i), j)
    copy = pltpu.make_async_copy(rows_ref.at[j], row_ref, sem)
    copy.start()
    copy.wait()


def pick_row(owner_rank, prefill_rows):
    return pl.pallas_call(
        pick_kernel,
        out_shape=jax.ShapeDtypeStruct(prefill_rows.shape[1:], prefill_rows.dtype),
        in_specs=[SMEM, HBM],
        out_specs=VMEM,
        scratch_shapes=[pltpu.SemaphoreType.DMA],
        compiler_params=pltpu.CompilerParams(vmem_limit_bytes=GRANT),
        name="pick_row",
    )(owner_rank, prefill_rows)


def cached_kernel(lengths_ref, cache_ref, row_ref, bias_ref, sem):
    mine = seat_request(cache_ref.shape[0])
    copy = pltpu.make_async_copy(cache_ref.at[mine], row_ref, sem)
    copy.start()
    position = lax.broadcasted_iota(jnp.int32, bias_ref.shape, 1)
    visible = (position < lengths_ref[mine]) | (position >= cache_ref.shape[1])
    bias_ref[...] = jnp.where(visible, 0.0, neg_fill)
    copy.wait()


def pick_cached(cached_lengths, latent_cache, positions):
    return pl.pallas_call(
        cached_kernel,
        out_shape=(
            jax.ShapeDtypeStruct(latent_cache.shape[1:], latent_cache.dtype),
            jax.ShapeDtypeStruct((8, positions), jnp.float32),
        ),
        in_specs=[SMEM, HBM],
        out_specs=(VMEM, VMEM),
        scratch_shapes=[pltpu.SemaphoreType.DMA],
        compiler_params=pltpu.CompilerParams(vmem_limit_bytes=GRANT),
        name="pick_cached",
    )(cached_lengths, latent_cache)


def project_kernel(
    both_hbm, up_hbm, out_proj_hbm, parts_hbm, both_ref, up_ref, weights, parts_ref, sems, out_sems
):
    n, _, columns = parts_ref.shape
    steps, _, wide = weights.shape
    each = wide // columns
    copies = [
        pltpu.make_async_copy(both_hbm, both_ref, sems.at[steps]),
        pltpu.make_async_copy(up_hbm, up_ref, sems.at[steps + 1]),
    ]
    for i in range(steps):
        window = out_proj_hbm.at[:, pl.ds(i * wide, wide)]
        copies.append(pltpu.make_async_copy(window, weights.at[i], sems.at[i]))
    for copy in copies:
        copy.start()
    copies[0].wait()
    copies[1].wait()
    both = both_ref[...]
    heads = [
        jnp.dot(both[:, i, :LAT], up_ref[i], preferred_element_type=jnp.float32)
        for i in range(up_ref.shape[0])
    ]
    head_out = jnp.concatenate(heads, axis=1).astype(jnp.bfloat16)
    seat = lax.broadcasted_iota(jnp.int32, (n, n), 1)
    request = lax.broadcasted_iota(jnp.int32, (n, n), 0)
    chip, core = lax.shift_right_logical(seat, 1), lax.bitwise_and(seat, 1)
    seat = n // 4 + chip + (n // 2) * core
    choose = lax.bitwise_and(request + lax.axis_index("ep") - seat, n - 1) == 0
    choose = jnp.where(choose, 1.0, 0.0).astype(jnp.bfloat16)
    head_out = jnp.dot(choose, head_out, preferred_element_type=jnp.float32).astype(jnp.bfloat16)
    sent = []
    for i in range(steps):
        copies[2 + i].wait()
        term = jnp.dot(head_out, weights[i], preferred_element_type=jnp.float32)
        for k in range(each):
            piece = term[:, k * columns : (k + 1) * columns]
            parts_ref[each * i + k] = piece.astype(jnp.bfloat16)
        done = pl.ds(each * i, each)
        sent.append(pltpu.make_async_copy(parts_ref.at[done], parts_hbm.at[done], out_sems.at[i]))
        sent[i].start()
    for copy in sent:
        copy.wait()


def project(both, value_up, out_proj):
    n = both.shape[0]
    depth, width = out_proj.shape
    steps = 4
    parts = jax.ShapeDtypeStruct((n, n, width // n), jnp.bfloat16)
    return pl.pallas_call(
        project_kernel,
        out_shape=parts,
        in_specs=[HBM, HBM, HBM],
        out_specs=HBM,
        scratch_shapes=[
            pltpu.VMEM(both.shape, both.dtype),
            pltpu.VMEM(value_up.shape, value_up.dtype),
            pltpu.VMEM((steps, depth, width // steps), out_proj.dtype),
            pltpu.VMEM(parts.shape, parts.dtype),
            pltpu.SemaphoreType.DMA((steps + 2,)),
            pltpu.SemaphoreType.DMA((steps,)),
        ],
        compiler_params=pltpu.CompilerParams(vmem_limit_bytes=GRANT),
        cost_estimate=pl.CostEstimate(
            flops=2 * n * depth * width, bytes_accessed=2 * depth * width, transcendentals=0
        ),
        name="project",
    )(both, value_up, out_proj)


def body(queries, latent_cache, cached_lengths, prefill_rows, owner_rank, value_up, out_proj):
    n = latent_cache.shape[0]
    width = latent_cache.shape[2]
    positions = latent_cache.shape[1] + prefill_rows.shape[1]
    d = lax.axis_index("ep")
    mine = seat_request(n)
    later, sooner = [], []
    for source in range(n):
        for k in range(n):
            owner = (sigma(k) - source) % n
            pair = (source * n + k, owner * n + k)
            (later if leaving(source, n) >= leaving(owner, n) else sooner).append(pair)
    from_later = leaving(mine, n) >= leaving(d, n)
    seats = jnp.array([sigma(k) for k in range(n)], dtype=jnp.int32)

    def choice():
        request_at = lax.rem(seats - d + n, n)
        return (request_at[:, None] == jnp.arange(n, dtype=jnp.int32)[None, :]).astype(jnp.bfloat16)

    def prepare(queries, cached_lengths, latent_cache):
        ordered = jnp.einsum("gr,rhk->ghk", choice(), queries, preferred_element_type=jnp.float32)
        q = lax.all_to_all(
            ordered.astype(jnp.bfloat16), ("hd", "rep"), split_axis=0, concat_axis=0, tiled=True
        )
        cache_row, bias = pick_cached(cached_lengths, latent_cache, positions)
        return q.reshape(-1, width), cache_row, bias

    def nothing(queries, cached_lengths, latent_cache):
        return (
            jnp.zeros((queries.shape[1] * n, width), queries.dtype),
            jnp.zeros(latent_cache.shape[1:], latent_cache.dtype),
            jnp.zeros((8, positions), jnp.float32),
        )

    early = d < n // 4
    row = pick_row(owner_rank, prefill_rows)
    operands = (queries, cached_lengths, latent_cache)
    late_row = lax.ppermute(row, ("ep", "hd", "rep"), later)
    had = lax.cond(early, prepare, nothing, *operands)
    early_row = lax.ppermute(row, ("ep", "hd", "rep"), sooner)
    q, cache_row, bias = lax.cond(
        early, lambda had, operands: had, lambda had, operands: prepare(*operands), had, operands
    )
    fresh_row = jnp.where(from_later, late_row, early_row)
    keys = jnp.concatenate([cache_row, fresh_row], axis=0)
    scores = jnp.einsum("hk,ck->hc", q, keys, preferred_element_type=jnp.float32) * score_scale
    scores = scores + bias[:1]
    maxima = jnp.max(scores, axis=-1, keepdims=True)
    weights = jnp.exp(scores - maxima)
    totals = jnp.sum(weights, axis=-1, keepdims=True)
    summed = jnp.einsum("hc,cl->hl", weights, keys[:, :LAT], preferred_element_type=jnp.float32)
    latent = (summed / totals).astype(jnp.bfloat16)
    latent = jnp.pad(latent, ((0, 0), (0, width - LAT)))
    both = jnp.concatenate([latent.reshape(n, 2, width), fresh_row.reshape(n, 2, width)], axis=1)
    both = lax.all_to_all(both, ("hd", "rep"), split_axis=0, concat_axis=0, tiled=True)
    parts = project(both, value_up, out_proj)
    arrived = lax.all_to_all(parts, ("hd", "rep"), split_axis=0, concat_axis=0, tiled=True)
    fresh = jnp.einsum("gr,ghk->rhk", choice(), both[:, 2:, :], preferred_element_type=jnp.float32)
    fresh = fresh.astype(jnp.bfloat16)
    mixed = arrived.astype(jnp.float32).sum(axis=0).astype(jnp.bfloat16)
    return (mixed, fresh)


def solution(mesh):
    in_specs = (
        P("ep", ("hd", "rep"), None),
        P("ep", None, None),
        P("ep"),
        P("ep", None, None),
        P("ep"),
        P(("hd", "rep"), None, None),
        P(("hd", "rep"), None),
    )
    out_specs = (P("ep", ("hd", "rep")), P("ep", ("hd", "rep"), None))

    return jax.shard_map(body, mesh=mesh, in_specs=in_specs, out_specs=out_specs, check_vma=False)
```

```python
import jax
import jax.numpy as jnp
from jax import lax
from jax.experimental import pallas as pl
from jax.experimental.pallas import tpu as pltpu
from jax.sharding import PartitionSpec as P


LAT = 512
score_scale = 192.0 ** (-0.5)
neg_fill = -1e30
GRANT = 64_720_000
VMEM = pl.BlockSpec(memory_space=pltpu.VMEM)
SMEM = pl.BlockSpec(memory_space=pltpu.SMEM)
HBM = pl.BlockSpec(memory_space=pltpu.HBM)


def sigma(g, n=32):
    return (n // 4 + g // 2 + n // 2 * (g % 2)) % n


def seat_request(n):
    d = lax.axis_index("ep")
    g = lax.axis_index("hd") * lax.axis_size("rep") + lax.axis_index("rep")
    seat = n // 4 + lax.div(g, 2) + (n // 2) * lax.rem(g, 2)
    return lax.rem(seat - d + n, n)


def leaving(z, n):
    half = n // 2
    rank = 12 * z * (z <= half) + (12 * half - 5 * (z - half)) * (z > half)
    return rank * n + z


def comes_first(source, owner, n):
    return (leaving(source, n) >= leaving(owner, n)) | ((source >= n // 4) & (owner >= n // 4))


def pick_kernel(owner_ref, rows_ref, row_ref, sem):
    n = rows_ref.shape[0]
    mine = seat_request(n)
    j = jnp.int32(0)
    for i in range(n):
        j = jnp.where(owner_ref[i] == mine, jnp.int32(i), j)
    copy = pltpu.make_async_copy(rows_ref.at[j], row_ref, sem)
    copy.start()
    copy.wait()


def pick_row(owner_rank, prefill_rows):
    return pl.pallas_call(
        pick_kernel,
        out_shape=jax.ShapeDtypeStruct(prefill_rows.shape[1:], prefill_rows.dtype),
        in_specs=[SMEM, HBM],
        out_specs=VMEM,
        scratch_shapes=[pltpu.SemaphoreType.DMA],
        compiler_params=pltpu.CompilerParams(vmem_limit_bytes=GRANT),
        name="pick_row",
    )(owner_rank, prefill_rows)


def cached_kernel(lengths_ref, cache_ref, row_ref, bias_ref, sem):
    mine = seat_request(cache_ref.shape[0])
    copy = pltpu.make_async_copy(cache_ref.at[mine], row_ref, sem)
    copy.start()
    position = lax.broadcasted_iota(jnp.int32, bias_ref.shape, 1)
    visible = (position < lengths_ref[mine]) | (position >= cache_ref.shape[1])
    bias_ref[...] = jnp.where(visible, 0.0, neg_fill)
    copy.wait()


def pick_cached(cached_lengths, latent_cache, positions):
    return pl.pallas_call(
        cached_kernel,
        out_shape=(
            jax.ShapeDtypeStruct(latent_cache.shape[1:], latent_cache.dtype),
            jax.ShapeDtypeStruct((8, positions), jnp.float32),
        ),
        in_specs=[SMEM, HBM],
        out_specs=(VMEM, VMEM),
        scratch_shapes=[pltpu.SemaphoreType.DMA],
        compiler_params=pltpu.CompilerParams(vmem_limit_bytes=GRANT),
        name="pick_cached",
    )(cached_lengths, latent_cache)


def project_kernel(
    both_hbm, up_hbm, out_proj_hbm, parts_hbm, both_ref, up_ref, weights, parts_ref, sems, out_sems
):
    n, _, columns = parts_ref.shape
    steps, _, wide = weights.shape
    each = wide // columns
    copies = [
        pltpu.make_async_copy(both_hbm, both_ref, sems.at[steps]),
        pltpu.make_async_copy(up_hbm, up_ref, sems.at[steps + 1]),
    ]
    for i in range(steps):
        window = out_proj_hbm.at[:, pl.ds(i * wide, wide)]
        copies.append(pltpu.make_async_copy(window, weights.at[i], sems.at[i]))
    for copy in copies:
        copy.start()
    copies[0].wait()
    copies[1].wait()
    both = both_ref[...]
    heads = [
        jnp.dot(both[:, i, :LAT], up_ref[i], preferred_element_type=jnp.float32)
        for i in range(up_ref.shape[0])
    ]
    head_out = jnp.concatenate(heads, axis=1).astype(jnp.bfloat16)
    seat = lax.broadcasted_iota(jnp.int32, (n, n), 1)
    request = lax.broadcasted_iota(jnp.int32, (n, n), 0)
    chip, core = lax.shift_right_logical(seat, 1), lax.bitwise_and(seat, 1)
    seat = n // 4 + chip + (n // 2) * core
    choose = lax.bitwise_and(request + lax.axis_index("ep") - seat, n - 1) == 0
    choose = jnp.where(choose, 1.0, 0.0).astype(jnp.bfloat16)
    head_out = jnp.dot(choose, head_out, preferred_element_type=jnp.float32).astype(jnp.bfloat16)
    sent = []
    for i in range(steps):
        copies[2 + i].wait()
        term = jnp.dot(head_out, weights[i], preferred_element_type=jnp.float32)
        for k in range(each):
            piece = term[:, k * columns : (k + 1) * columns]
            parts_ref[each * i + k] = piece.astype(jnp.bfloat16)
        done = pl.ds(each * i, each)
        sent.append(pltpu.make_async_copy(parts_ref.at[done], parts_hbm.at[done], out_sems.at[i]))
        sent[i].start()
    for copy in sent:
        copy.wait()


def project(both, value_up, out_proj):
    n = both.shape[0]
    depth, width = out_proj.shape
    steps = 4
    parts = jax.ShapeDtypeStruct((n, n, width // n), jnp.bfloat16)
    return pl.pallas_call(
        project_kernel,
        out_shape=parts,
        in_specs=[HBM, HBM, HBM],
        out_specs=HBM,
        scratch_shapes=[
            pltpu.VMEM(both.shape, both.dtype),
            pltpu.VMEM(value_up.shape, value_up.dtype),
            pltpu.VMEM((steps, depth, width // steps), out_proj.dtype),
            pltpu.VMEM(parts.shape, parts.dtype),
            pltpu.SemaphoreType.DMA((steps + 2,)),
            pltpu.SemaphoreType.DMA((steps,)),
        ],
        compiler_params=pltpu.CompilerParams(vmem_limit_bytes=GRANT),
        cost_estimate=pl.CostEstimate(
            flops=2 * n * depth * width, bytes_accessed=2 * depth * width, transcendentals=0
        ),
        name="project",
    )(both, value_up, out_proj)


def body(queries, latent_cache, cached_lengths, prefill_rows, owner_rank, value_up, out_proj):
    n = latent_cache.shape[0]
    width = latent_cache.shape[2]
    positions = latent_cache.shape[1] + prefill_rows.shape[1]
    d = lax.axis_index("ep")
    mine = seat_request(n)
    later, sooner = [], []
    for source in range(n):
        for k in range(n):
            owner = (sigma(k) - source) % n
            pair = (source * n + k, owner * n + k)
            (later if comes_first(source, owner, n) else sooner).append(pair)
    from_later = comes_first(mine, d, n)
    seats = jnp.array([sigma(k) for k in range(n)], dtype=jnp.int32)

    def choice():
        request_at = lax.rem(seats - d + n, n)
        return (request_at[:, None] == jnp.arange(n, dtype=jnp.int32)[None, :]).astype(jnp.bfloat16)

    def prepare(queries, cached_lengths, latent_cache):
        ordered = jnp.einsum("gr,rhk->ghk", choice(), queries, preferred_element_type=jnp.float32)
        q = lax.all_to_all(
            ordered.astype(jnp.bfloat16), ("hd", "rep"), split_axis=0, concat_axis=0, tiled=True
        )
        cache_row, bias = pick_cached(cached_lengths, latent_cache, positions)
        return q.reshape(-1, width), cache_row, bias

    def nothing(queries, cached_lengths, latent_cache):
        return (
            jnp.zeros((queries.shape[1] * n, width), queries.dtype),
            jnp.zeros(latent_cache.shape[1:], latent_cache.dtype),
            jnp.zeros((8, positions), jnp.float32),
        )

    early = d < n // 4
    row = pick_row(owner_rank, prefill_rows)
    operands = (queries, cached_lengths, latent_cache)
    late_row = lax.ppermute(row, ("ep", "hd", "rep"), later)
    had = lax.cond(early, prepare, nothing, *operands)
    early_row = lax.ppermute(row, ("ep", "hd", "rep"), sooner)
    q, cache_row, bias = lax.cond(
        early, lambda had, operands: had, lambda had, operands: prepare(*operands), had, operands
    )
    fresh_row = jnp.where(from_later, late_row, early_row)
    keys = jnp.concatenate([cache_row, fresh_row], axis=0)
    scores = jnp.einsum("hk,ck->hc", q, keys, preferred_element_type=jnp.float32) * score_scale
    scores = scores + bias[:1]
    maxima = jnp.max(scores, axis=-1, keepdims=True)
    weights = jnp.exp(scores - maxima)
    totals = jnp.sum(weights, axis=-1, keepdims=True)
    summed = jnp.einsum("hc,cl->hl", weights, keys[:, :LAT], preferred_element_type=jnp.float32)
    latent = (summed / totals).astype(jnp.bfloat16)
    latent = jnp.pad(latent, ((0, 0), (0, width - LAT)))
    both = jnp.concatenate([latent.reshape(n, 2, width), fresh_row.reshape(n, 2, width)], axis=1)
    both = lax.all_to_all(both, ("hd", "rep"), split_axis=0, concat_axis=0, tiled=True)
    parts = project(both, value_up, out_proj)
    arrived = lax.all_to_all(parts, ("hd", "rep"), split_axis=0, concat_axis=0, tiled=True)
    fresh = jnp.einsum("gr,ghk->rhk", choice(), both[:, 2:, :], preferred_element_type=jnp.float32)
    fresh = fresh.astype(jnp.bfloat16)
    mixed = arrived.astype(jnp.float32).sum(axis=0).astype(jnp.bfloat16)
    return (mixed, fresh)


def solution(mesh):
    in_specs = (
        P("ep", ("hd", "rep"), None),
        P("ep", None, None),
        P("ep"),
        P("ep", None, None),
        P("ep"),
        P(("hd", "rep"), None, None),
        P(("hd", "rep"), None),
    )
    out_specs = (P("ep", ("hd", "rep")), P("ep", ("hd", "rep"), None))

    return jax.shard_map(body, mesh=mesh, in_specs=in_specs, out_specs=out_specs, check_vma=False)
```

```python
import jax
import jax.numpy as jnp
from jax import lax
from jax.experimental import pallas as pl
from jax.experimental.pallas import tpu as pltpu
from jax.sharding import PartitionSpec as P


LAT = 512
score_scale = 192.0 ** (-0.5)
neg_fill = -1e30
GRANT = 64_720_000
VMEM = pl.BlockSpec(memory_space=pltpu.VMEM)
SMEM = pl.BlockSpec(memory_space=pltpu.SMEM)
HBM = pl.BlockSpec(memory_space=pltpu.HBM)


def sigma(g, n=32):
    return (n // 4 + (g // 2 + n // 8) % (n // 2) + n // 2 * (g % 2)) % n


def seat_request(n):
    d = lax.axis_index("ep")
    g = lax.axis_index("hd") * lax.axis_size("rep") + lax.axis_index("rep")
    seat = n // 4 + lax.rem(lax.div(g, 2) + n // 8, n // 2) + (n // 2) * lax.rem(g, 2)
    return lax.rem(seat - d + n, n)


def leaving(z, n):
    half = n // 2
    rank = 12 * z * (z <= half) + (12 * half - 5 * (z - half)) * (z > half)
    return rank * n + z


def comes_first(source, owner, n):
    return (leaving(source, n) >= leaving(owner, n)) & ((source < n // 4) | (owner < n // 4))


def pick_kernel(owner_ref, rows_ref, row_ref, sem):
    n = rows_ref.shape[0]
    mine = seat_request(n)
    j = jnp.int32(0)
    for i in range(n):
        j = jnp.where(owner_ref[i] == mine, jnp.int32(i), j)
    copy = pltpu.make_async_copy(rows_ref.at[j], row_ref, sem)
    copy.start()
    copy.wait()


def pick_row(owner_rank, prefill_rows):
    return pl.pallas_call(
        pick_kernel,
        out_shape=jax.ShapeDtypeStruct(prefill_rows.shape[1:], prefill_rows.dtype),
        in_specs=[SMEM, HBM],
        out_specs=VMEM,
        scratch_shapes=[pltpu.SemaphoreType.DMA],
        compiler_params=pltpu.CompilerParams(vmem_limit_bytes=GRANT),
        name="pick_row",
    )(owner_rank, prefill_rows)


def cached_kernel(lengths_ref, cache_ref, row_ref, bias_ref, sem):
    mine = seat_request(cache_ref.shape[0])
    copy = pltpu.make_async_copy(cache_ref.at[mine], row_ref, sem)
    copy.start()
    position = lax.broadcasted_iota(jnp.int32, bias_ref.shape, 1)
    visible = (position < lengths_ref[mine]) | (position >= cache_ref.shape[1])
    bias_ref[...] = jnp.where(visible, 0.0, neg_fill)
    copy.wait()


def pick_cached(cached_lengths, latent_cache, positions):
    return pl.pallas_call(
        cached_kernel,
        out_shape=(
            jax.ShapeDtypeStruct(latent_cache.shape[1:], latent_cache.dtype),
            jax.ShapeDtypeStruct((8, positions), jnp.float32),
        ),
        in_specs=[SMEM, HBM],
        out_specs=(VMEM, VMEM),
        scratch_shapes=[pltpu.SemaphoreType.DMA],
        compiler_params=pltpu.CompilerParams(vmem_limit_bytes=GRANT),
        name="pick_cached",
    )(cached_lengths, latent_cache)


def project_kernel(
    both_hbm, up_hbm, out_proj_hbm, parts_hbm, both_ref, up_ref, weights, parts_ref, sems, out_sems
):
    n, _, columns = parts_ref.shape
    steps, _, wide = weights.shape
    each = wide // columns
    copies = [
        pltpu.make_async_copy(both_hbm, both_ref, sems.at[steps]),
        pltpu.make_async_copy(up_hbm, up_ref, sems.at[steps + 1]),
    ]
    for i in range(steps):
        window = out_proj_hbm.at[:, pl.ds(i * wide, wide)]
        copies.append(pltpu.make_async_copy(window, weights.at[i], sems.at[i]))
    for copy in copies:
        copy.start()
    copies[0].wait()
    copies[1].wait()
    both = both_ref[...]
    heads = [
        jnp.dot(both[:, i, :LAT], up_ref[i], preferred_element_type=jnp.float32)
        for i in range(up_ref.shape[0])
    ]
    head_out = jnp.concatenate(heads, axis=1).astype(jnp.bfloat16)
    seat = lax.broadcasted_iota(jnp.int32, (n, n), 1)
    request = lax.broadcasted_iota(jnp.int32, (n, n), 0)
    chip, core = lax.shift_right_logical(seat, 1), lax.bitwise_and(seat, 1)
    seat = n // 4 + lax.bitwise_and(chip + n // 8, n // 2 - 1) + (n // 2) * core
    choose = lax.bitwise_and(request + lax.axis_index("ep") - seat, n - 1) == 0
    choose = jnp.where(choose, 1.0, 0.0).astype(jnp.bfloat16)
    head_out = jnp.dot(choose, head_out, preferred_element_type=jnp.float32).astype(jnp.bfloat16)
    sent = []
    for i in range(steps):
        copies[2 + i].wait()
        term = jnp.dot(head_out, weights[i], preferred_element_type=jnp.float32)
        for k in range(each):
            piece = term[:, k * columns : (k + 1) * columns]
            parts_ref[each * i + k] = piece.astype(jnp.bfloat16)
        done = pl.ds(each * i, each)
        sent.append(pltpu.make_async_copy(parts_ref.at[done], parts_hbm.at[done], out_sems.at[i]))
        sent[i].start()
    for copy in sent:
        copy.wait()


def project(both, value_up, out_proj):
    n = both.shape[0]
    depth, width = out_proj.shape
    steps = 4
    parts = jax.ShapeDtypeStruct((n, n, width // n), jnp.bfloat16)
    return pl.pallas_call(
        project_kernel,
        out_shape=parts,
        in_specs=[HBM, HBM, HBM],
        out_specs=HBM,
        scratch_shapes=[
            pltpu.VMEM(both.shape, both.dtype),
            pltpu.VMEM(value_up.shape, value_up.dtype),
            pltpu.VMEM((steps, depth, width // steps), out_proj.dtype),
            pltpu.VMEM(parts.shape, parts.dtype),
            pltpu.SemaphoreType.DMA((steps + 2,)),
            pltpu.SemaphoreType.DMA((steps,)),
        ],
        compiler_params=pltpu.CompilerParams(vmem_limit_bytes=GRANT),
        cost_estimate=pl.CostEstimate(
            flops=2 * n * depth * width, bytes_accessed=2 * depth * width, transcendentals=0
        ),
        name="project",
    )(both, value_up, out_proj)


def body(queries, latent_cache, cached_lengths, prefill_rows, owner_rank, value_up, out_proj):
    n = latent_cache.shape[0]
    width = latent_cache.shape[2]
    positions = latent_cache.shape[1] + prefill_rows.shape[1]
    d = lax.axis_index("ep")
    mine = seat_request(n)
    later, sooner = [], []
    for source in range(n):
        for k in range(n):
            owner = (sigma(k) - source) % n
            pair = (source * n + k, owner * n + k)
            (later if comes_first(source, owner, n) else sooner).append(pair)
    from_later = comes_first(mine, d, n)
    seats = jnp.array([sigma(k) for k in range(n)], dtype=jnp.int32)

    def choice():
        request_at = lax.rem(seats - d + n, n)
        return (request_at[:, None] == jnp.arange(n, dtype=jnp.int32)[None, :]).astype(jnp.bfloat16)

    def prepare(queries, cached_lengths, latent_cache):
        ordered = jnp.einsum("gr,rhk->ghk", choice(), queries, preferred_element_type=jnp.float32)
        q = lax.all_to_all(
            ordered.astype(jnp.bfloat16), ("hd", "rep"), split_axis=0, concat_axis=0, tiled=True
        )
        cache_row, bias = pick_cached(cached_lengths, latent_cache, positions)
        return q.reshape(-1, width), cache_row, bias

    def nothing(queries, cached_lengths, latent_cache):
        return (
            jnp.zeros((queries.shape[1] * n, width), queries.dtype),
            jnp.zeros(latent_cache.shape[1:], latent_cache.dtype),
            jnp.zeros((8, positions), jnp.float32),
        )

    early = d < n // 4
    row = pick_row(owner_rank, prefill_rows)
    operands = (queries, cached_lengths, latent_cache)
    late_row = lax.ppermute(row, ("ep", "hd", "rep"), later)
    had = lax.cond(early, prepare, nothing, *operands)
    early_row = lax.ppermute(row, ("ep", "hd", "rep"), sooner)
    q, cache_row, bias = lax.cond(
        early, lambda had, operands: had, lambda had, operands: prepare(*operands), had, operands
    )
    fresh_row = jnp.where(from_later, late_row, early_row)
    keys = jnp.concatenate([cache_row, fresh_row], axis=0)
    scores = jnp.einsum("hk,ck->hc", q, keys, preferred_element_type=jnp.float32) * score_scale
    scores = scores + bias[:1]
    maxima = jnp.max(scores, axis=-1, keepdims=True)
    weights = jnp.exp(scores - maxima)
    totals = jnp.sum(weights, axis=-1, keepdims=True)
    summed = jnp.einsum("hc,cl->hl", weights, keys[:, :LAT], preferred_element_type=jnp.float32)
    latent = (summed / totals).astype(jnp.bfloat16)
    latent = jnp.pad(latent, ((0, 0), (0, width - LAT)))
    both = jnp.concatenate([latent.reshape(n, 2, width), fresh_row.reshape(n, 2, width)], axis=1)
    both = lax.all_to_all(both, ("hd", "rep"), split_axis=0, concat_axis=0, tiled=True)
    parts = project(both, value_up, out_proj)
    arrived = lax.all_to_all(parts, ("hd", "rep"), split_axis=0, concat_axis=0, tiled=True)
    fresh = jnp.einsum("gr,ghk->rhk", choice(), both[:, 2:, :], preferred_element_type=jnp.float32)
    fresh = fresh.astype(jnp.bfloat16)
    mixed = arrived.astype(jnp.float32).sum(axis=0).astype(jnp.bfloat16)
    return (mixed, fresh)


def solution(mesh):
    in_specs = (
        P("ep", ("hd", "rep"), None),
        P("ep", None, None),
        P("ep"),
        P("ep", None, None),
        P("ep"),
        P(("hd", "rep"), None, None),
        P(("hd", "rep"), None),
    )
    out_specs = (P("ep", ("hd", "rep")), P("ep", ("hd", "rep"), None))

    return jax.shard_map(body, mesh=mesh, in_specs=in_specs, out_specs=out_specs, check_vma=False)
```
